32 devices in a mesh: depth: 2 (over x), wide: 16 (over z, y, core).
Axes of the slice: x: 2, y: 2, z: 4, core: 2. Of those that a mesh axis runs over, the one named last changes fastest.
Arguments:
- volume: bfloat16 [256, 128, 1024], P(('depth', 'wide')), may hold values from -6 to 6
- directions: int32 [2, 128], replicated, may hold values from 0 to 1
- light_dir: float32 [2, 3], replicated, may hold values from -4 to 4
- tf_center: float32 [2, 4], replicated, may hold values from -1.5 to 1.5
- tf_width: float32 [2, 4], replicated, may hold values from 0.2 to 0.8
- tf_height: float32 [2, 4], replicated, may hold values from 0.25 to 4
- tf_emission: float32 [2, 4, 3], replicated, may hold values from 0.5 to 6
Outputs:
- image_rgba: float32 [2, 4, 131072], P(None, None, ('depth', 'wide'))
The draws below stay inside these ranges and needn't reach their ends.
Inputs may be any that keep to these rules, and one draw needn't show every extreme that they name: `directions`: 0 marks rays that run toward increasing depth index, 1 rays that run toward decreasing depth index.
All inputs are finite; a program needn't handle non-finite values.
Results may differ from the reference program's by a relative error of at most 0.0003.
Values may be sent and summed in bfloat16 or wider, within the bound.
A program may use at most 64 MiB of HBM per device.

```python
import math
import jax
import jax.numpy as jnp
from jax import lax

IW = 1024
IH = 128
VIEWS = 2
BUMPS = 4
NZ = 256


def place_ends(drawn, key, low, high):
    spot = [jax.random.randint(jax.random.fold_in(key, axis), (), 0, length) for axis, length in enumerate(drawn.shape)]
    main_axis = drawn.shape.index(max(drawn.shape))
    beside = spot[:main_axis] + [(spot[main_axis] + 1) % drawn.shape[main_axis]] + spot[main_axis + 1:]
    return drawn.at[tuple(spot)].set(low).at[tuple(beside)].set(high)


def steps_of(rng, shape, cuts, low, largest):
    def one(position, parts):
        heights = jax.random.uniform(jax.random.fold_in(jax.random.fold_in(rng, 6), position), (parts,), jnp.float32, low / len(cuts), largest / len(cuts))
        return jnp.repeat(jnp.exp(heights), shape[position] // parts).reshape((-1,) + (1,) * (len(shape) - position - 1))

    level = one(*cuts[0])
    for cut in cuts[1:]:
        level = level * one(*cut)
    return level


def centred(key, dims, deviation, reach, cuts=(), held_as=jnp.bfloat16):
    array = deviation * jax.random.normal(key, dims, jnp.float32)
    if cuts:
        array = array * steps_of(key, dims, cuts, -0.22, 0.18)
    return jnp.clip(array, -reach, reach).astype(held_as)


def setup_inputs(seed: int = 0) -> dict:
    streams_of = jax.random.split(jax.random.key(seed), 8)
    return {
        "volume": centred(streams_of[0], (NZ, IH, IW), 1.0, 6.0, ((0, 32),)),
        "directions": place_ends(jax.random.randint(streams_of[1], (VIEWS, IH), 0, 2), jax.random.fold_in(streams_of[1], 1), 0, 1).astype(jnp.int32),
        "light_dir": centred(streams_of[2], (VIEWS, 3), 1.0, 4.0, (), jnp.float32),
        "tf_center": jnp.clip(jax.random.uniform(streams_of[3], (VIEWS, BUMPS), jnp.float32, -1.5, 1.5), -1.5, 1.5),
        "tf_width": jnp.clip(jax.random.uniform(streams_of[4], (VIEWS, BUMPS), jnp.float32, 0.2, 0.8), 0.2, 0.8),
        "tf_height": jnp.clip(jnp.exp(jax.random.uniform(streams_of[5], (VIEWS, BUMPS), jnp.float32, math.log(0.25), math.log(4.0))), 0.25, 4.0),
        "tf_emission": jnp.clip(jax.random.uniform(streams_of[6], (VIEWS, BUMPS, 3), jnp.float32, 0.5, 6.0), 0.5, 6.0),
    }


AMBIENT = 0.3
DIFFUSE = 0.7

def shifted_diff(values, along_axis):
    padding = [(0, 0)] * values.ndim
    padding[along_axis] = (1, 1)
    padded = jnp.pad(values, padding)
    length_now = values.shape[along_axis]
    upper_part = lax.slice_in_dim(padded, 2, length_now + 2, 1, along_axis)
    lower_part = lax.slice_in_dim(padded, 0, length_now, 1, along_axis)
    return 0.5 * (upper_part - lower_part)

def layer_rgba(layer_below, center_layer, layer_above, light_dir, tf_center, tf_width, tf_height, tf_emission, depth_step):
    grad_z = 0.5 * (layer_above - layer_below)
    grad_y = shifted_diff(center_layer, 0)
    grad_x = shifted_diff(center_layer, 1)
    lighting = jnp.abs(grad_z[None] * light_dir[:, 0, None, None] + grad_y[None] * light_dir[:, 1, None, None] + grad_x[None] * light_dir[:, 2, None, None])
    magnitude = jnp.sqrt(grad_x * grad_x + grad_y * grad_y + grad_z * grad_z + 1.0)
    shading = AMBIENT + DIFFUSE * lighting / magnitude[None]
    scaled = (center_layer[None, None] - tf_center[:, :, None, None]) / tf_width[:, :, None, None]
    bumps = jnp.exp(-scaled * scaled)
    density = lax.optimization_barrier(jnp.sum(tf_height[:, :, None, None] * bumps, axis=1))
    weights = tf_height[:, :, None] * tf_emission
    tinted = jnp.einsum('vkc,vkhw->vchw', weights, bumps, precision=lax.Precision.HIGHEST)
    colour = depth_step * shading[:, None] * tinted
    opacity = 1.0 - jnp.exp(-depth_step * density)
    sample_rgba = jnp.concatenate([colour, opacity[:, None]], axis=1)
    return sample_rgba.reshape(sample_rgba.shape[0], 4, -1)

def over_ordered(lower_part, upper_part, flags):
    front_first = lower_part + (1.0 - lower_part[:, 3:4]) * upper_part
    back_first = upper_part + (1.0 - upper_part[:, 3:4]) * lower_part
    return jnp.where(flags, back_first, front_first)

def reference(volume, directions, light_dir, tf_center, tf_width, tf_height, tf_emission):
    layer_total = volume.shape[0]
    depth_step = 1.0 / layer_total
    padded = jnp.pad(volume, ((1, 1), (0, 0), (0, 0)))
    flags = jnp.repeat(directions == 1, volume.shape[2], axis=1)[:, None, :]

    def advance(composite, layer_index):
        layers = lax.dynamic_slice_in_dim(padded, layer_index, 3, 0).astype(jnp.float32)
        sample_rgba = layer_rgba(layers[0], layers[1], layers[2], light_dir, tf_center, tf_width, tf_height, tf_emission, depth_step)
        return (over_ordered(composite, sample_rgba, flags), None)
    initial = jnp.zeros((light_dir.shape[0], 4, volume.shape[1] * volume.shape[2]), jnp.float32)
    composite, unused = lax.scan(advance, initial, jnp.arange(layer_total, dtype=jnp.int32))
    return composite
```

```python
import functools
import math

import jax
import jax.numpy as jnp
from jax import lax
from jax.experimental import pallas as pl
from jax.experimental.pallas import tpu as pltpu
from jax.sharding import PartitionSpec as P

AMBIENT = 0.3
DIFFUSE = 0.7


def padded_2(block, sides, width):
    for axis, dim in sides:
        count = lax.axis_size(axis)
        forward = [(i, i + 1) for i in range(count - 1)]
        backward = [(target, source) for source, target in forward]
        low = lax.ppermute(
            lax.slice_in_dim(block, block.shape[dim] - width, None, axis=dim), axis, forward
        )
        high = lax.ppermute(lax.slice_in_dim(block, 0, width, axis=dim), axis, backward)
        block = jnp.concatenate([low, block, high], axis=dim)
    return block


def partner(block, axis, distance):
    count = lax.axis_size(axis)
    route = []
    for low in range(count):
        high = low | 1 << distance
        if high != low and high < count:
            route += [(low, high), (high, low)]
    return lax.ppermute(block, axis, route)


def shifted_diff(values, along_axis):
    padding = [(0, 0)] * values.ndim
    padding[along_axis] = (1, 1)
    padded = jnp.pad(values, padding)
    length_now = values.shape[along_axis]
    upper_part = lax.slice_in_dim(padded, 2, length_now + 2, 1, along_axis)
    lower_part = lax.slice_in_dim(padded, 0, length_now, 1, along_axis)
    return 0.5 * (upper_part - lower_part)


def layer_rgba(
    layer_below,
    center_layer,
    layer_above,
    light_dir,
    tf_center,
    tf_width,
    tf_height,
    tf_emission,
    depth_step,
):
    grad_z = 0.5 * (layer_above - layer_below)
    grad_y = shifted_diff(center_layer, 0)
    grad_x = shifted_diff(center_layer, 1)
    lighting = jnp.abs(
        grad_z[None] * light_dir[:, 0, None, None]
        + grad_y[None] * light_dir[:, 1, None, None]
        + grad_x[None] * light_dir[:, 2, None, None]
    )
    magnitude = jnp.sqrt(grad_x * grad_x + grad_y * grad_y + grad_z * grad_z + 1.0)
    shading = AMBIENT + DIFFUSE * lighting / magnitude[None]
    scaled = (center_layer[None, None] - tf_center[:, :, None, None]) / tf_width[:, :, None, None]
    bumps = jnp.exp(-scaled * scaled)
    density = jnp.sum(tf_height[:, :, None, None] * bumps, axis=1)
    weights = tf_height[:, :, None] * tf_emission
    tinted = jnp.einsum("vkc,vkhw->vchw", weights, bumps, precision=lax.Precision.HIGHEST)
    colour = depth_step * shading[:, None] * tinted
    opacity = 1.0 - jnp.exp(-depth_step * density)
    sample_rgba = jnp.concatenate([colour, opacity[:, None]], axis=1)
    return sample_rgba.reshape(sample_rgba.shape[0], 4, -1)


def over_ordered(lower_part, upper_part, flags):
    front_first = lower_part + (1.0 - lower_part[:, 3:4]) * upper_part
    back_first = upper_part + (1.0 - upper_part[:, 3:4]) * lower_part
    return jnp.where(flags, back_first, front_first)


def split_pair(values, along_axis):
    array_shape = values.shape
    new_shape = (
        array_shape[:along_axis] + (array_shape[along_axis] // 2, 2) + array_shape[along_axis + 1 :]
    )
    paired = values.reshape(new_shape)
    first_half = lax.index_in_dim(paired, 0, along_axis + 1, keepdims=False)
    second_half = lax.index_in_dim(paired, 1, along_axis + 1, keepdims=False)
    return (first_half, second_half)


def plain_body(volume, directions, light_dir, tf_center, tf_width, tf_height, tf_emission):
    depth_count = lax.axis_size("depth")
    wide_count = lax.axis_size("wide")
    slab_cells = volume.shape[0]
    depth_step = 1.0 / (slab_cells * depth_count * wide_count)
    view_count = light_dir.shape[0]
    pixel_count = volume.shape[1] * volume.shape[2]
    flags = jnp.repeat(directions == 1, volume.shape[2], axis=1)[:, None, :]
    padded = padded_2(volume, ((("depth", "wide"), 0),), 1)

    def advance(layer_index, composite):
        layers = lax.dynamic_slice_in_dim(padded, layer_index, 3, 0).astype(jnp.float32)
        sample_rgba = layer_rgba(
            layers[0],
            layers[1],
            layers[2],
            light_dir,
            tf_center,
            tf_width,
            tf_height,
            tf_emission,
            depth_step,
        )
        return over_ordered(composite, sample_rgba, flags)

    initial = jnp.zeros((view_count, 4, pixel_count), jnp.float32)
    slab_image = lax.fori_loop(0, slab_cells, advance, initial)
    block_pixels = pixel_count // (depth_count * wide_count)
    blocked = slab_image.reshape(view_count, 4, depth_count, wide_count, block_pixels)
    blocked_flags = flags.reshape(view_count, 1, depth_count, wide_count, block_pixels)
    wide_index = lax.axis_index("wide")
    depth_index = lax.axis_index("depth")
    merged = blocked
    merged_flags = blocked_flags
    for bit_number in range(wide_count.bit_length() - 1):
        own_bit = wide_index >> bit_number & 1
        first_half, second_half = split_pair(merged, 3)
        flag_first, flag_second = split_pair(merged_flags, 3)
        kept = jnp.where(own_bit == 0, first_half, second_half)
        outgoing = jnp.where(own_bit == 0, second_half, first_half)
        merged_flags = jnp.where(own_bit == 0, flag_first, flag_second)
        incoming = partner(outgoing, "wide", bit_number)
        merged = jnp.where(
            own_bit == 0,
            over_ordered(kept, incoming, merged_flags),
            over_ordered(incoming, kept, merged_flags),
        )
    range_image = jnp.squeeze(merged, 3)
    range_flags = jnp.squeeze(merged_flags, 3)
    merged = range_image
    merged_flags = range_flags
    for bit_number in range(depth_count.bit_length() - 1):
        own_bit = depth_index >> bit_number & 1
        first_half, second_half = split_pair(merged, 2)
        flag_first, flag_second = split_pair(merged_flags, 2)
        kept = jnp.where(own_bit == 0, first_half, second_half)
        outgoing = jnp.where(own_bit == 0, second_half, first_half)
        merged_flags = jnp.where(own_bit == 0, flag_first, flag_second)
        incoming = partner(outgoing, "depth", bit_number)
        merged = jnp.where(
            own_bit == 0,
            over_ordered(kept, incoming, merged_flags),
            over_ordered(incoming, kept, merged_flags),
        )
    final_block = jnp.squeeze(merged, 2)
    return final_block


MESH = pl.DeviceIdType.MESH
LOG2E = math.log2(math.e)
LANES = 256
ROWS = 16
LAG_CORE, LAG_Y, LAG_Z0, LAG_Z1, LAG_X = 2, 5, 8, 12, 15


def kernel(
    layer_total, chunks, groups,
    vol, dirs, light, center, width, height, tint,
    out,
    xf, halo, flagv, cst, obuf, cbuf, ysend, ybuf, zbuf, wbuf, xbuf, fin,
    halo_ss, halo_rs, send_sem, recv_sem, fin_ss, fin_rs,
):
    slab, rows, cols = vol.shape
    step = 1.0 / layer_total
    x = lax.axis_index("depth")
    w = lax.axis_index("wide")
    c = lax.rem(w, 2)
    y = lax.rem(lax.div(w, 2), 2)
    z0 = lax.rem(lax.div(w, 4), 2)
    z1 = lax.div(w, 8)
    me = x * 16 + w
    peers = (
        (x, w + 1 - 2 * c),
        (x, w + 2 - 4 * y),
        (x, w + 4 - 8 * z0),
        (x, w + 8 - 16 * z1),
        (1 - x, w),
    )
    core_peer, y_peer, z0_peer, z1_peer, x_peer = peers
    after = lax.rem(me + 1, 32)
    before = lax.rem(me + 31, 32)
    next_dev = (lax.div(after, 16), lax.rem(after, 16))
    prev_dev = (lax.div(before, 16), lax.rem(before, 16))
    has_prev = me > 0
    has_next = me < 31

    barrier = pltpu.get_barrier_semaphore()
    for peer in peers + (next_dev, prev_dev):
        pl.semaphore_signal(barrier, inc=1, device_id=peer, device_id_type=MESH)
    pl.semaphore_wait(barrier, 7)

    quarters = cols // LANES

    def up_copy(q):
        return pltpu.make_async_remote_copy(
            src_ref=vol.at[slab - 1, :, pl.ds(pl.multiple_of(q * LANES, LANES), LANES)],
            dst_ref=halo.at[0, q], send_sem=halo_ss.at[0, q], recv_sem=halo_rs.at[0, q],
            device_id=next_dev, device_id_type=MESH)

    def down_copy(q):
        return pltpu.make_async_remote_copy(
            src_ref=vol.at[0, :, pl.ds(pl.multiple_of(q * LANES, LANES), LANES)],
            dst_ref=halo.at[1, q], send_sem=halo_ss.at[1, q], recv_sem=halo_rs.at[1, q],
            device_id=prev_dev, device_id_type=MESH)

    for q in range(quarters):
        @pl.when(has_next)
        def _():
            up_copy(q).start()

        @pl.when(has_prev)
        def _():
            down_copy(q).start()

    for v in range(2):
        for k in range(4):
            full = lambda ref: jnp.full((8, 128), ref[v, k], jnp.float32)
            scale = math.sqrt(LOG2E) / full(width)
            cst[v * 15 + k] = scale
            cst[v * 15 + 4 + k] = scale * full(center)
            cst[v * 15 + 8 + k] = jnp.log(full(height) * (step * LOG2E)) * LOG2E
        for a in range(3):
            cst[v * 15 + 12 + a] = jnp.full((8, 128), DIFFUSE * light[v, a], jnp.float32)
    row_of = lax.broadcasted_iota(jnp.int32, (8, 128), 0)
    lane_of = lax.broadcasted_iota(jnp.int32, (8, 128), 1)

    def fill_flags(g, carry):
        for v in range(2):
            value = jnp.zeros((8, 128), jnp.float32)
            for i in range(8):
                value = jnp.where(row_of == i, dirs[v, g * 8 + i].astype(jnp.float32), value)
            flagv[v, g] = value
        return carry

    lax.fori_loop(0, rows // 8, fill_flags, 0)

    def pad(z, carry):
        xf[z, 0:8, :] = jnp.zeros((8, cols + 256), jnp.float32)
        xf[z, rows + 8:rows + 16, :] = jnp.zeros((8, cols + 256), jnp.float32)
        xf[z, 8:rows + 8, 0:128] = jnp.zeros((rows, 128), jnp.float32)
        xf[z, 8:rows + 8, cols + 128:cols + 256] = jnp.zeros((rows, 128), jnp.float32)

        def widen(b, inner):
            xf[z, pl.ds(pl.multiple_of(b * 16 + 8, 8), 16), 128:cols + 128] = vol[
                z - 1, pl.ds(pl.multiple_of(b * 16, 16), 16), :
            ].astype(jnp.float32)
            return inner

        return lax.fori_loop(0, rows // 16, widen, carry)

    lax.fori_loop(1, slab + 1, pad, 0)

    def take_halo(side, place, present, copy, q):
        lanes = pl.ds(pl.multiple_of(q * LANES + 128, 128), LANES)

        @pl.when(present)
        def _():
            copy(q).wait_recv()
            xf[place, 8:rows + 8, lanes] = halo[side, q].astype(jnp.float32)

        @pl.when(jnp.logical_not(present))
        def _():
            xf[place, 8:rows + 8, lanes] = jnp.zeros((rows, LANES), jnp.float32)

    def place_of(k):
        return lax.rem(k, groups), lax.div(k, groups)

    def render(k):
        j, q = place_of(k)

        def tile(t, carry):
            h = lax.div(t, 2)
            p = lax.rem(t, 2)
            g = j * 2 + h
            r0 = pl.multiple_of(g * 8 + 8, 8)
            l0 = pl.multiple_of(q * LANES + p * 128 + 128, 128)
            here_rows, here_lanes = pl.ds(r0, 8), pl.ds(l0, 128)
            flags = [flagv[v, g] > 0.5 for v in range(2)]
            signs = [jnp.where(f, 1.0, -1.0) for f in flags]
            run = [jnp.zeros((8, 128), jnp.float32)] * 2
            sums = [[jnp.zeros((8, 128), jnp.float32)] * 4 for v in range(2)]
            for z in range(1, slab + 1):
                here = xf[z, here_rows, here_lanes]
                left = xf[z, here_rows, pl.ds(pl.multiple_of(l0 - 128, 128), 128)]
                right = xf[z, here_rows, pl.ds(pl.multiple_of(l0 + 128, 128), 128)]
                above = xf[z, pl.ds(pl.multiple_of(r0 - 8, 8), 8), here_lanes]
                below = xf[z, pl.ds(pl.multiple_of(r0 + 8, 8), 8), here_lanes]
                gz = xf[z + 1, here_rows, here_lanes] - xf[z - 1, here_rows, here_lanes]
                gx = pltpu.roll(jnp.where(lane_of == 0, right, here), 127, 1) - pltpu.roll(
                    jnp.where(lane_of == 127, left, here), 1, 1)
                gy = pltpu.roll(jnp.where(row_of == 0, below, here), 7, 0) - pltpu.roll(
                    jnp.where(row_of == 7, above, here), 1, 0)
                inverse = lax.rsqrt(gx * gx + gy * gy + (gz * gz + 4.0))
                for v in range(2):
                    dot = gz * cst[v * 15 + 12] + gy * cst[v * 15 + 13] + gx * cst[v * 15 + 14]
                    shade = jnp.abs(dot) * inverse + AMBIENT
                    bumps = []
                    for b in range(4):
                        u = here * cst[v * 15 + b] - cst[v * 15 + 4 + b]
                        bumps.append(jnp.exp2(cst[v * 15 + 8 + b] - u * u))
                    thick = (bumps[0] + bumps[1]) + (bumps[2] + bumps[3])
                    later = run[v] + signs[v] * thick
                    weight = jnp.exp2(jnp.where(flags[v], later, run[v])) * shade
                    run[v] = later
                    sums[v] = [s + weight * b for s, b in zip(sums[v], bumps)]
            lanes = pl.ds(pl.multiple_of(p * 128, 128), 128)
            for v in range(2):
                clear = jnp.exp2(-signs[v] * run[v])
                front = jnp.where(flags[v], clear, 1.0)
                scaled = [s * front for s in sums[v]]
                parts = []
                for ch in range(3):
                    total = scaled[0] * (tint[v, 0, ch] * (1.0 / LOG2E))
                    for b in range(1, 4):
                        total = total + scaled[b] * (tint[v, b, ch] * (1.0 / LOG2E))
                    parts.append(total)
                parts.append(clear)

                @pl.when(c == v)
                def _():
                    for ch in range(4):
                        cbuf[c, k, h, ch, :, lanes] = parts[ch]

                @pl.when(c != v)
                def _():
                    for ch in range(4):
                        obuf[k, h, ch, :, lanes] = parts[ch]
            return carry

        lax.fori_loop(0, 4, tile, 0)

    def merged(low, high, flag):
        lt, ut = low(3), high(3)
        p = jnp.where(flag, ut, 1.0)
        o = jnp.where(flag, 1.0, lt)
        return [p * low(ch) + o * high(ch) for ch in range(3)] + [lt * ut]

    def merge(low, high, flag_tile, store):
        for p in range(LANES // 128):
            s = slice(p * 128, p * 128 + 128)
            parts = merged(lambda ch: low[ch, :, s], lambda ch: high[ch, :, s], flag_tile > 0.5)
            for ch in range(4):
                store[ch, :, s] = parts[ch]

    def core_copy(k):
        return pltpu.make_async_remote_copy(
            src_ref=obuf.at[k], dst_ref=cbuf.at[c, k], send_sem=send_sem.at[0, k],
            recv_sem=recv_sem.at[0, k], device_id=core_peer, device_id_type=MESH)

    def y_copy(k):
        return pltpu.make_async_remote_copy(
            src_ref=ysend.at[k], dst_ref=ybuf.at[y, k], send_sem=send_sem.at[1, k],
            recv_sem=recv_sem.at[1, k], device_id=y_peer, device_id_type=MESH)

    def pass_on(buf, bit, stage, peer):
        return lambda k: pltpu.make_async_remote_copy(
            src_ref=buf.at[bit, k], dst_ref=buf.at[bit, k], send_sem=send_sem.at[stage, k],
            recv_sem=recv_sem.at[stage, k], device_id=peer, device_id_type=MESH)

    z0_copy = pass_on(zbuf, z0, 2, z0_peer)
    z1_copy = pass_on(wbuf, z1, 3, z1_peer)
    x_copy = pass_on(xbuf, x, 4, x_peer)

    def bits(k):
        j = lax.rem(k, groups)
        return lax.rem(j, 2), lax.rem(lax.div(j, 2), 2), lax.div(j, 4)

    def held(k):
        b0, b1, bx = bits(k)
        at0 = b0 == z0
        at1 = jnp.logical_and(at0, b1 == z1)
        return at0, at1, jnp.logical_and(at1, bx == x)

    def group_flag(k, half):
        return flagv[c, lax.rem(k, groups) * 2 + half]

    def inside(i, lag):
        return jnp.logical_and(i >= lag, i < chunks + lag)

    def advance(i, carry):
        @pl.when(jnp.logical_and(i < chunks, lax.rem(i, groups) == 0))
        def _():
            q = lax.div(i, groups)
            take_halo(0, 0, has_prev, up_copy, q)
            take_halo(1, slab + 1, has_next, down_copy, q)

        @pl.when(i < chunks)
        def _():
            render(i)
            core_copy(i).start()

        @pl.when(inside(i, LAG_CORE))
        def _():
            k = i - LAG_CORE
            core_copy(k).wait_recv()
            merge(cbuf.at[0, k, 1 - y], cbuf.at[1, k, 1 - y], group_flag(k, 1 - y), ysend.at[k])
            y_copy(k).start()
            merge(cbuf.at[0, k, y], cbuf.at[1, k, y], group_flag(k, y), ybuf.at[y, k])

        @pl.when(inside(i, LAG_Y))
        def _():
            k = i - LAG_Y
            y_copy(k).wait_recv()
            merge(ybuf.at[0, k], ybuf.at[1, k], group_flag(k, y), zbuf.at[z0, k])

            @pl.when(jnp.logical_not(held(k)[0]))
            def _():
                z0_copy(k).start()

        @pl.when(jnp.logical_and(inside(i, LAG_Z0), held(i + groups * 4 - LAG_Z0)[0]))
        def _():
            k = i - LAG_Z0
            z0_copy(k).wait_recv()
            merge(zbuf.at[0, k], zbuf.at[1, k], group_flag(k, y), wbuf.at[z1, k])

            @pl.when(jnp.logical_not(held(k)[1]))
            def _():
                z1_copy(k).start()

        @pl.when(jnp.logical_and(inside(i, LAG_Z1), held(i + groups * 4 - LAG_Z1)[1]))
        def _():
            k = i - LAG_Z1
            z1_copy(k).wait_recv()
            merge(wbuf.at[0, k], wbuf.at[1, k], group_flag(k, y), xbuf.at[x, k])

            @pl.when(jnp.logical_not(held(k)[2]))
            def _():
                x_copy(k).start()

        @pl.when(jnp.logical_and(inside(i, LAG_X), held(i + groups * 4 - LAG_X)[2]))
        def _():
            k = i - LAG_X
            x_copy(k).wait_recv()
            flag = group_flag(k, y) > 0.5
            for p in range(LANES // 128):
                s = slice(p * 128, p * 128 + 128)
                parts = merged(lambda ch: xbuf[0, k, ch, :, s], lambda ch: xbuf[1, k, ch, :, s], flag)
                parts[3] = 1.0 - parts[3]
                for r in range(8):
                    start = (r % 4) * cols + lax.div(k, groups) * LANES + p * 128
                    spot = pl.ds(pl.multiple_of(start, 128), 128)
                    for ch in range(4):
                        fin[r // 4, ch:ch + 1, spot] = parts[ch][r:r + 1, :]

        return carry

    lax.fori_loop(0, chunks + LAG_X, advance, 0)

    last = pltpu.make_async_remote_copy(
        src_ref=fin.at[1 - c], dst_ref=out.at[c], send_sem=fin_ss, recv_sem=fin_rs,
        device_id=core_peer, device_id_type=MESH)
    last.start()
    out[c] = fin[c]

    def settle(k, carry):
        core_copy(k).wait_send()
        y_copy(k).wait_send()
        at0, at1, at2 = held(k)

        @pl.when(jnp.logical_not(at0))
        def _():
            z0_copy(k).wait_send()

        @pl.when(jnp.logical_and(at0, jnp.logical_not(at1)))
        def _():
            z1_copy(k).wait_send()

        @pl.when(jnp.logical_and(at1, jnp.logical_not(at2)))
        def _():
            x_copy(k).wait_send()

        return carry

    lax.fori_loop(0, chunks, settle, 0)
    for q in range(quarters):
        @pl.when(has_next)
        def _():
            up_copy(q).wait_send()

        @pl.when(has_prev)
        def _():
            down_copy(q).wait_send()
    last.wait()


def fused_body(volume, directions, light_dir, tf_center, tf_width, tf_height, tf_emission):
    slab, rows, cols = volume.shape
    devices = lax.axis_size("depth") * lax.axis_size("wide")
    quarters = cols // LANES
    groups = rows // ROWS
    chunks = groups * quarters
    f32 = jnp.float32
    piece = (4, 8, LANES)
    vmem = pl.BlockSpec(memory_space=pltpu.VMEM)
    smem = pl.BlockSpec(memory_space=pltpu.SMEM)
    return pl.pallas_call(
        functools.partial(kernel, slab * devices, chunks, groups),
        out_shape=jax.ShapeDtypeStruct((2, 4, rows * cols // devices), f32),
        in_specs=[vmem] + [smem] * 6,
        out_specs=vmem,
        scratch_shapes=[
            pltpu.VMEM((slab + 2, rows + 16, cols + 256), f32),
            pltpu.VMEM((2, quarters, rows, LANES), volume.dtype),
            pltpu.VMEM((2, rows // 8, 8, 128), f32),
            pltpu.VMEM((30, 8, 128), f32),
            pltpu.VMEM((chunks, 2) + piece, f32),
            pltpu.VMEM((2, chunks, 2) + piece, f32),
            pltpu.VMEM((chunks,) + piece, f32),
            pltpu.VMEM((2, chunks) + piece, f32),
            pltpu.VMEM((2, chunks) + piece, f32),
            pltpu.VMEM((2, chunks) + piece, f32),
            pltpu.VMEM((2, chunks) + piece, f32),
            pltpu.VMEM((2, 4, rows * cols // devices), f32),
            pltpu.SemaphoreType.DMA((2, quarters)),
            pltpu.SemaphoreType.DMA((2, quarters)),
            pltpu.SemaphoreType.DMA((5, chunks)),
            pltpu.SemaphoreType.DMA((5, chunks)),
            pltpu.SemaphoreType.DMA,
            pltpu.SemaphoreType.DMA,
        ],
        compiler_params=pltpu.CompilerParams(
            collective_id=0, has_side_effects=True, vmem_limit_bytes=48 * 1024 * 1024
        ),
    )(volume, directions, light_dir, tf_center, tf_width, tf_height, tf_emission)


def body(volume, *parameters):
    slab, rows, cols = volume.shape
    fused = (
        lax.axis_size("depth") == 2
        and lax.axis_size("wide") == 16
        and rows == 128
        and cols % LANES == 0
    )
    return (fused_body if fused else plain_body)(volume, *parameters)


def solution(mesh):
    return jax.shard_map(
        body,
        mesh=mesh,
        in_specs=(P(("depth", "wide"), None, None), P(), P(), P(), P(), P(), P()),
        out_specs=P(None, None, ("depth", "wide")),
        check_vma=False,
    )
```

```python
import functools
import math

import jax
import jax.numpy as jnp
from jax import lax
from jax.experimental import pallas as pl
from jax.experimental.pallas import tpu as pltpu
from jax.sharding import PartitionSpec as P

AMBIENT = 0.3
DIFFUSE = 0.7


def padded_2(block, sides, width):
    for axis, dim in sides:
        count = lax.axis_size(axis)
        forward = [(i, i + 1) for i in range(count - 1)]
        backward = [(target, source) for source, target in forward]
        low = lax.ppermute(
            lax.slice_in_dim(block, block.shape[dim] - width, None, axis=dim), axis, forward
        )
        high = lax.ppermute(lax.slice_in_dim(block, 0, width, axis=dim), axis, backward)
        block = jnp.concatenate([low, block, high], axis=dim)
    return block


def partner(block, axis, distance):
    count = lax.axis_size(axis)
    route = []
    for low in range(count):
        high = low | 1 << distance
        if high != low and high < count:
            route += [(low, high), (high, low)]
    return lax.ppermute(block, axis, route)


def shifted_diff(values, along_axis):
    padding = [(0, 0)] * values.ndim
    padding[along_axis] = (1, 1)
    padded = jnp.pad(values, padding)
    length_now = values.shape[along_axis]
    upper_part = lax.slice_in_dim(padded, 2, length_now + 2, 1, along_axis)
    lower_part = lax.slice_in_dim(padded, 0, length_now, 1, along_axis)
    return 0.5 * (upper_part - lower_part)


def layer_rgba(
    layer_below,
    center_layer,
    layer_above,
    light_dir,
    tf_center,
    tf_width,
    tf_height,
    tf_emission,
    depth_step,
):
    grad_z = 0.5 * (layer_above - layer_below)
    grad_y = shifted_diff(center_layer, 0)
    grad_x = shifted_diff(center_layer, 1)
    lighting = jnp.abs(
        grad_z[None] * light_dir[:, 0, None, None]
        + grad_y[None] * light_dir[:, 1, None, None]
        + grad_x[None] * light_dir[:, 2, None, None]
    )
    magnitude = jnp.sqrt(grad_x * grad_x + grad_y * grad_y + grad_z * grad_z + 1.0)
    shading = AMBIENT + DIFFUSE * lighting / magnitude[None]
    scaled = (center_layer[None, None] - tf_center[:, :, None, None]) / tf_width[:, :, None, None]
    bumps = jnp.exp(-scaled * scaled)
    density = jnp.sum(tf_height[:, :, None, None] * bumps, axis=1)
    weights = tf_height[:, :, None] * tf_emission
    tinted = jnp.einsum("vkc,vkhw->vchw", weights, bumps, precision=lax.Precision.HIGHEST)
    colour = depth_step * shading[:, None] * tinted
    opacity = 1.0 - jnp.exp(-depth_step * density)
    sample_rgba = jnp.concatenate([colour, opacity[:, None]], axis=1)
    return sample_rgba.reshape(sample_rgba.shape[0], 4, -1)


def over_ordered(lower_part, upper_part, flags):
    front_first = lower_part + (1.0 - lower_part[:, 3:4]) * upper_part
    back_first = upper_part + (1.0 - upper_part[:, 3:4]) * lower_part
    return jnp.where(flags, back_first, front_first)


def split_pair(values, along_axis):
    array_shape = values.shape
    new_shape = (
        array_shape[:along_axis] + (array_shape[along_axis] // 2, 2) + array_shape[along_axis + 1 :]
    )
    paired = values.reshape(new_shape)
    first_half = lax.index_in_dim(paired, 0, along_axis + 1, keepdims=False)
    second_half = lax.index_in_dim(paired, 1, along_axis + 1, keepdims=False)
    return (first_half, second_half)


def plain_body(volume, directions, light_dir, tf_center, tf_width, tf_height, tf_emission):
    depth_count = lax.axis_size("depth")
    wide_count = lax.axis_size("wide")
    slab_cells = volume.shape[0]
    depth_step = 1.0 / (slab_cells * depth_count * wide_count)
    view_count = light_dir.shape[0]
    pixel_count = volume.shape[1] * volume.shape[2]
    flags = jnp.repeat(directions == 1, volume.shape[2], axis=1)[:, None, :]
    padded = padded_2(volume, ((("depth", "wide"), 0),), 1)

    def advance(layer_index, composite):
        layers = lax.dynamic_slice_in_dim(padded, layer_index, 3, 0).astype(jnp.float32)
        sample_rgba = layer_rgba(
            layers[0],
            layers[1],
            layers[2],
            light_dir,
            tf_center,
            tf_width,
            tf_height,
            tf_emission,
            depth_step,
        )
        return over_ordered(composite, sample_rgba, flags)

    initial = jnp.zeros((view_count, 4, pixel_count), jnp.float32)
    slab_image = lax.fori_loop(0, slab_cells, advance, initial)
    block_pixels = pixel_count // (depth_count * wide_count)
    blocked = slab_image.reshape(view_count, 4, depth_count, wide_count, block_pixels)
    blocked_flags = flags.reshape(view_count, 1, depth_count, wide_count, block_pixels)
    wide_index = lax.axis_index("wide")
    depth_index = lax.axis_index("depth")
    merged = blocked
    merged_flags = blocked_flags
    for bit_number in range(wide_count.bit_length() - 1):
        own_bit = wide_index >> bit_number & 1
        first_half, second_half = split_pair(merged, 3)
        flag_first, flag_second = split_pair(merged_flags, 3)
        kept = jnp.where(own_bit == 0, first_half, second_half)
        outgoing = jnp.where(own_bit == 0, second_half, first_half)
        merged_flags = jnp.where(own_bit == 0, flag_first, flag_second)
        incoming = partner(outgoing, "wide", bit_number)
        merged = jnp.where(
            own_bit == 0,
            over_ordered(kept, incoming, merged_flags),
            over_ordered(incoming, kept, merged_flags),
        )
    range_image = jnp.squeeze(merged, 3)
    range_flags = jnp.squeeze(merged_flags, 3)
    merged = range_image
    merged_flags = range_flags
    for bit_number in range(depth_count.bit_length() - 1):
        own_bit = depth_index >> bit_number & 1
        first_half, second_half = split_pair(merged, 2)
        flag_first, flag_second = split_pair(merged_flags, 2)
        kept = jnp.where(own_bit == 0, first_half, second_half)
        outgoing = jnp.where(own_bit == 0, second_half, first_half)
        merged_flags = jnp.where(own_bit == 0, flag_first, flag_second)
        incoming = partner(outgoing, "depth", bit_number)
        merged = jnp.where(
            own_bit == 0,
            over_ordered(kept, incoming, merged_flags),
            over_ordered(incoming, kept, merged_flags),
        )
    final_block = jnp.squeeze(merged, 2)
    return final_block


MESH = pl.DeviceIdType.MESH
LOG2E = math.log2(math.e)
LANES = 256
ROWS = 16
LAG_CORE, LAG_Y, LAG_Z0, LAG_Z1, LAG_X = 3, 8, 13, 18, 22


def kernel(
    layer_total, chunks, groups,
    vol, dirs_in, light_in, center_in, width_in, height_in, tint_in,
    out,
    slabs, dirs, light, center, width, height, tint, in_sems,
    xf, halo, flagv, cst, obuf, cbuf, ysend, ybuf, zbuf, wbuf, xbuf, fin,
    halo_ss, halo_rs, send_sem, recv_sem, fin_ss, fin_rs,
):
    slab, rows, cols = vol.shape
    step = 1.0 / layer_total
    x = lax.axis_index("depth")
    w = lax.axis_index("wide")
    c = lax.rem(w, 2)
    y = lax.rem(lax.div(w, 2), 2)
    z0 = lax.rem(lax.div(w, 4), 2)
    z1 = lax.div(w, 8)
    me = x * 16 + w
    peers = (
        (x, w + 1 - 2 * c),
        (x, w + 2 - 4 * y),
        (x, w + 4 - 8 * z0),
        (x, w + 8 - 16 * z1),
        (1 - x, w),
    )
    core_peer, y_peer, z0_peer, z1_peer, x_peer = peers
    after = lax.rem(me + 1, 32)
    before = lax.rem(me + 31, 32)
    next_dev = (lax.div(after, 16), lax.rem(after, 16))
    prev_dev = (lax.div(before, 16), lax.rem(before, 16))
    has_prev = me > 0
    has_next = me < 31

    given = (
        (dirs_in, dirs), (light_in, light), (center_in, center), (width_in, width),
        (height_in, height), (tint_in, tint),
    )
    small = [pltpu.make_async_copy(a, b, in_sems.at[n]) for n, (a, b) in enumerate(given)]

    def slab_copy(z):
        return pltpu.make_async_copy(vol.at[z], slabs.at[z], in_sems.at[6 + z])

    barrier = pltpu.get_barrier_semaphore()
    for peer in peers + (next_dev, prev_dev):
        pl.semaphore_signal(barrier, inc=1, device_id=peer, device_id_type=MESH)
    for copy in small:
        copy.start()
    for z in range(slab):
        slab_copy(z).start()
    pl.semaphore_wait(barrier, 7)

    quarters = cols // LANES

    def up_copy(q):
        return pltpu.make_async_remote_copy(
            src_ref=vol.at[slab - 1, :, pl.ds(pl.multiple_of(q * LANES, LANES), LANES)],
            dst_ref=halo.at[0, q], send_sem=halo_ss.at[0, q], recv_sem=halo_rs.at[0, q],
            device_id=next_dev, device_id_type=MESH)

    def down_copy(q):
        return pltpu.make_async_remote_copy(
            src_ref=vol.at[0, :, pl.ds(pl.multiple_of(q * LANES, LANES), LANES)],
            dst_ref=halo.at[1, q], send_sem=halo_ss.at[1, q], recv_sem=halo_rs.at[1, q],
            device_id=prev_dev, device_id_type=MESH)

    for q in range(quarters):
        @pl.when(has_next)
        def _():
            up_copy(q).start()

        @pl.when(has_prev)
        def _():
            down_copy(q).start()

    for copy in small:
        copy.wait()
    for v in range(2):
        for k in range(4):
            full = lambda ref: jnp.full((8, 128), ref[v, k], jnp.float32)
            scale = math.sqrt(LOG2E) / full(width)
            cst[v * 15 + k] = scale
            cst[v * 15 + 4 + k] = scale * full(center)
            cst[v * 15 + 8 + k] = jnp.log(full(height) * (step * LOG2E)) * LOG2E
        for a in range(3):
            cst[v * 15 + 12 + a] = jnp.full((8, 128), DIFFUSE * light[v, a], jnp.float32)
    row_of = lax.broadcasted_iota(jnp.int32, (8, 128), 0)
    lane_of = lax.broadcasted_iota(jnp.int32, (8, 128), 1)

    def fill_flags(g, carry):
        for v in range(2):
            value = jnp.zeros((8, 128), jnp.float32)
            for i in range(8):
                value = jnp.where(row_of == i, dirs[v, g * 8 + i].astype(jnp.float32), value)
            flagv[v, g] = value
        return carry

    lax.fori_loop(0, rows // 8, fill_flags, 0)

    def pad(z, carry):
        slab_copy(z - 1).wait()
        xf[z, 0:8, :] = jnp.zeros((8, cols + 256), jnp.float32)
        xf[z, rows + 8:rows + 16, :] = jnp.zeros((8, cols + 256), jnp.float32)
        xf[z, 8:rows + 8, 0:128] = jnp.zeros((rows, 128), jnp.float32)
        xf[z, 8:rows + 8, cols + 128:cols + 256] = jnp.zeros((rows, 128), jnp.float32)

        def widen(b, inner):
            xf[z, pl.ds(pl.multiple_of(b * 16 + 8, 8), 16), 128:cols + 128] = slabs[
                z - 1, pl.ds(pl.multiple_of(b * 16, 16), 16), :
            ].astype(jnp.float32)
            return inner

        return lax.fori_loop(0, rows // 16, widen, carry)

    lax.fori_loop(1, slab + 1, pad, 0)

    def take_halo(side, place, present, copy, q):
        lanes = pl.ds(pl.multiple_of(q * LANES + 128, 128), LANES)

        @pl.when(present)
        def _():
            copy(q).wait_recv()
            xf[place, 8:rows + 8, lanes] = halo[side, q].astype(jnp.float32)

        @pl.when(jnp.logical_not(present))
        def _():
            xf[place, 8:rows + 8, lanes] = jnp.zeros((rows, LANES), jnp.float32)

    def place_of(k):
        return lax.rem(k, groups), lax.div(k, groups)

    def render(k):
        j, q = place_of(k)

        def tile(t, carry):
            h = lax.div(t, 2)
            p = lax.rem(t, 2)
            g = j * 2 + h
            r0 = pl.multiple_of(g * 8 + 8, 8)
            l0 = pl.multiple_of(q * LANES + p * 128 + 128, 128)
            here_rows, here_lanes = pl.ds(r0, 8), pl.ds(l0, 128)
            flags = [flagv[v, g] > 0.5 for v in range(2)]
            signs = [jnp.where(f, 1.0, -1.0) for f in flags]
            run = [jnp.zeros((8, 128), jnp.float32)] * 2
            sums = [[jnp.zeros((8, 128), jnp.float32)] * 4 for v in range(2)]
            for z in range(1, slab + 1):
                here = xf[z, here_rows, here_lanes]
                left = xf[z, here_rows, pl.ds(pl.multiple_of(l0 - 128, 128), 128)]
                right = xf[z, here_rows, pl.ds(pl.multiple_of(l0 + 128, 128), 128)]
                above = xf[z, pl.ds(pl.multiple_of(r0 - 8, 8), 8), here_lanes]
                below = xf[z, pl.ds(pl.multiple_of(r0 + 8, 8), 8), here_lanes]
                gz = xf[z + 1, here_rows, here_lanes] - xf[z - 1, here_rows, here_lanes]
                gx = pltpu.roll(jnp.where(lane_of == 0, right, here), 127, 1) - pltpu.roll(
                    jnp.where(lane_of == 127, left, here), 1, 1)
                gy = pltpu.roll(jnp.where(row_of == 0, below, here), 7, 0) - pltpu.roll(
                    jnp.where(row_of == 7, above, here), 1, 0)
                inverse = lax.rsqrt(gx * gx + gy * gy + (gz * gz + 4.0))
                for v in range(2):
                    dot = gz * cst[v * 15 + 12] + gy * cst[v * 15 + 13] + gx * cst[v * 15 + 14]
                    shade = jnp.abs(dot) * inverse + AMBIENT
                    bumps = []
                    for b in range(4):
                        u = here * cst[v * 15 + b] - cst[v * 15 + 4 + b]
                        bumps.append(jnp.exp2(cst[v * 15 + 8 + b] - u * u))
                    thick = (bumps[0] + bumps[1]) + (bumps[2] + bumps[3])
                    later = run[v] + signs[v] * thick
                    weight = jnp.exp2(jnp.where(flags[v], later, run[v])) * shade
                    run[v] = later
                    sums[v] = [s + weight * b for s, b in zip(sums[v], bumps)]
            lanes = pl.ds(pl.multiple_of(p * 128, 128), 128)
            for v in range(2):
                clear = jnp.exp2(-signs[v] * run[v])
                front = jnp.where(flags[v], clear, 1.0)
                scaled = [s * front for s in sums[v]]
                parts = []
                for ch in range(3):
                    total = scaled[0] * (tint[ch, v, 0] * (1.0 / LOG2E))
                    for b in range(1, 4):
                        total = total + scaled[b] * (tint[ch, v, b] * (1.0 / LOG2E))
                    parts.append(total)
                parts.append(clear)

                @pl.when(c == v)
                def _():
                    for ch in range(4):
                        cbuf[c, k, h, ch, :, lanes] = parts[ch]

                @pl.when(c != v)
                def _():
                    for ch in range(4):
                        obuf[k, h, ch, :, lanes] = parts[ch]
            return carry

        lax.fori_loop(0, 4, tile, 0)

    def merged(low, high, flag):
        lt, ut = low(3), high(3)
        p = jnp.where(flag, ut, 1.0)
        o = jnp.where(flag, 1.0, lt)
        return [p * low(ch) + o * high(ch) for ch in range(3)] + [lt * ut]

    def merge(low, high, flag_tile, store):
        for p in range(LANES // 128):
            s = slice(p * 128, p * 128 + 128)
            parts = merged(lambda ch: low[ch, :, s], lambda ch: high[ch, :, s], flag_tile > 0.5)
            for ch in range(4):
                store[ch, :, s] = parts[ch]

    def core_copy(k):
        return pltpu.make_async_remote_copy(
            src_ref=obuf.at[k], dst_ref=cbuf.at[c, k], send_sem=send_sem.at[0, k],
            recv_sem=recv_sem.at[0, k], device_id=core_peer, device_id_type=MESH)

    def y_copy(k):
        return pltpu.make_async_remote_copy(
            src_ref=ysend.at[k], dst_ref=ybuf.at[y, k], send_sem=send_sem.at[1, k],
            recv_sem=recv_sem.at[1, k], device_id=y_peer, device_id_type=MESH)

    def pass_on(buf, bit, stage, peer):
        return lambda k: pltpu.make_async_remote_copy(
            src_ref=buf.at[bit, k], dst_ref=buf.at[bit, k], send_sem=send_sem.at[stage, k],
            recv_sem=recv_sem.at[stage, k], device_id=peer, device_id_type=MESH)

    z0_copy = pass_on(zbuf, z0, 2, z0_peer)
    z1_copy = pass_on(wbuf, z1, 3, z1_peer)
    x_copy = pass_on(xbuf, x, 4, x_peer)

    def bits(k):
        j = lax.rem(k, groups)
        return lax.rem(j, 2), lax.rem(lax.div(j, 2), 2), lax.div(j, 4)

    def held(k):
        b0, b1, bx = bits(k)
        at0 = b0 == z0
        at1 = jnp.logical_and(at0, b1 == z1)
        return at0, at1, jnp.logical_and(at1, bx == x)

    def group_flag(k, half):
        return flagv[c, lax.rem(k, groups) * 2 + half]

    def inside(i, lag):
        return jnp.logical_and(i >= lag, i < chunks + lag)

    def advance(i, carry):
        @pl.when(jnp.logical_and(i < chunks, lax.rem(i, groups) == 0))
        def _():
            q = lax.div(i, groups)
            take_halo(0, 0, has_prev, up_copy, q)
            take_halo(1, slab + 1, has_next, down_copy, q)

        @pl.when(i < chunks)
        def _():
            render(i)
            core_copy(i).start()

        @pl.when(inside(i, LAG_CORE))
        def _():
            k = i - LAG_CORE
            core_copy(k).wait_recv()
            merge(cbuf.at[0, k, 1 - y], cbuf.at[1, k, 1 - y], group_flag(k, 1 - y), ysend.at[k])
            y_copy(k).start()
            merge(cbuf.at[0, k, y], cbuf.at[1, k, y], group_flag(k, y), ybuf.at[y, k])

        @pl.when(inside(i, LAG_Y))
        def _():
            k = i - LAG_Y
            y_copy(k).wait_recv()
            merge(ybuf.at[0, k], ybuf.at[1, k], group_flag(k, y), zbuf.at[z0, k])

            @pl.when(jnp.logical_not(held(k)[0]))
            def _():
                z0_copy(k).start()

        @pl.when(jnp.logical_and(inside(i, LAG_Z0), held(i + groups * 4 - LAG_Z0)[0]))
        def _():
            k = i - LAG_Z0
            z0_copy(k).wait_recv()
            merge(zbuf.at[0, k], zbuf.at[1, k], group_flag(k, y), wbuf.at[z1, k])

            @pl.when(jnp.logical_not(held(k)[1]))
            def _():
                z1_copy(k).start()

        @pl.when(jnp.logical_and(inside(i, LAG_Z1), held(i + groups * 4 - LAG_Z1)[1]))
        def _():
            k = i - LAG_Z1
            z1_copy(k).wait_recv()
            merge(wbuf.at[0, k], wbuf.at[1, k], group_flag(k, y), xbuf.at[x, k])

            @pl.when(jnp.logical_not(held(k)[2]))
            def _():
                x_copy(k).start()

        @pl.when(jnp.logical_and(inside(i, LAG_X), held(i + groups * 4 - LAG_X)[2]))
        def _():
            k = i - LAG_X
            x_copy(k).wait_recv()
            flag = group_flag(k, y) > 0.5
            for p in range(LANES // 128):
                s = slice(p * 128, p * 128 + 128)
                parts = merged(lambda ch: xbuf[0, k, ch, :, s], lambda ch: xbuf[1, k, ch, :, s], flag)
                parts[3] = 1.0 - parts[3]
                for r in range(8):
                    start = (r % 4) * cols + lax.div(k, groups) * LANES + p * 128
                    spot = pl.ds(pl.multiple_of(start, 128), 128)
                    for ch in range(4):
                        fin[r // 4, ch:ch + 1, spot] = parts[ch][r:r + 1, :]

        return carry

    lax.fori_loop(0, chunks + LAG_X, advance, 0)

    last = pltpu.make_async_remote_copy(
        src_ref=fin.at[1 - c], dst_ref=out.at[c], send_sem=fin_ss, recv_sem=fin_rs,
        device_id=core_peer, device_id_type=MESH)
    last.start()
    out[c] = fin[c]

    def settle(k, carry):
        core_copy(k).wait_send()
        y_copy(k).wait_send()
        at0, at1, at2 = held(k)

        @pl.when(jnp.logical_not(at0))
        def _():
            z0_copy(k).wait_send()

        @pl.when(jnp.logical_and(at0, jnp.logical_not(at1)))
        def _():
            z1_copy(k).wait_send()

        @pl.when(jnp.logical_and(at1, jnp.logical_not(at2)))
        def _():
            x_copy(k).wait_send()

        return carry

    lax.fori_loop(0, chunks, settle, 0)
    for q in range(quarters):
        @pl.when(has_next)
        def _():
            up_copy(q).wait_send()

        @pl.when(has_prev)
        def _():
            down_copy(q).wait_send()
    last.wait()


def fused_body(volume, directions, light_dir, tf_center, tf_width, tf_height, tf_emission):
    slab, rows, cols = volume.shape
    devices = lax.axis_size("depth") * lax.axis_size("wide")
    quarters = cols // LANES
    groups = rows // ROWS
    chunks = groups * quarters
    f32 = jnp.float32
    piece = (4, 8, LANES)
    vmem = pl.BlockSpec(memory_space=pltpu.VMEM)
    hbm = pl.BlockSpec(memory_space=pltpu.HBM)
    parameters = (
        directions, light_dir, tf_center, tf_width, tf_height, jnp.transpose(tf_emission, (2, 0, 1))
    )
    return pl.pallas_call(
        functools.partial(kernel, slab * devices, chunks, groups),
        out_shape=jax.ShapeDtypeStruct((2, 4, rows * cols // devices), f32),
        in_specs=[hbm] * 7,
        out_specs=vmem,
        scratch_shapes=[pltpu.VMEM(volume.shape, volume.dtype)]
        + [pltpu.SMEM(p.shape, p.dtype) for p in parameters]
        + [
            pltpu.SemaphoreType.DMA((6 + slab,)),
            pltpu.VMEM((slab + 2, rows + 16, cols + 256), f32),
            pltpu.VMEM((2, quarters, rows, LANES), volume.dtype),
            pltpu.VMEM((2, rows // 8, 8, 128), f32),
            pltpu.VMEM((30, 8, 128), f32),
            pltpu.VMEM((chunks, 2) + piece, f32),
            pltpu.VMEM((2, chunks, 2) + piece, f32),
            pltpu.VMEM((chunks,) + piece, f32),
            pltpu.VMEM((2, chunks) + piece, f32),
            pltpu.VMEM((2, chunks) + piece, f32),
            pltpu.VMEM((2, chunks) + piece, f32),
            pltpu.VMEM((2, chunks) + piece, f32),
            pltpu.VMEM((2, 4, rows * cols // devices), f32),
            pltpu.SemaphoreType.DMA((2, quarters)),
            pltpu.SemaphoreType.DMA((2, quarters)),
            pltpu.SemaphoreType.DMA((5, chunks)),
            pltpu.SemaphoreType.DMA((5, chunks)),
            pltpu.SemaphoreType.DMA,
            pltpu.SemaphoreType.DMA,
        ],
        compiler_params=pltpu.CompilerParams(
            collective_id=0, has_side_effects=True, vmem_limit_bytes=67043328
        ),
    )(volume, *parameters)


def body(volume, *parameters):
    slab, rows, cols = volume.shape
    fused = (
        lax.axis_size("depth") == 2
        and lax.axis_size("wide") == 16
        and rows == 128
        and cols % LANES == 0
    )
    return (fused_body if fused else plain_body)(volume, *parameters)


def solution(mesh):
    return jax.shard_map(
        body,
        mesh=mesh,
        in_specs=(P(("depth", "wide"), None, None), P(), P(), P(), P(), P(), P()),
        out_specs=P(None, None, ("depth", "wide")),
        check_vma=False,
    )
```

```python
import functools
import math

import jax
import jax.numpy as jnp
from jax import lax
from jax.experimental import pallas as pl
from jax.experimental.pallas import tpu as pltpu
from jax.sharding import PartitionSpec as P

AMBIENT = 0.3
DIFFUSE = 0.7


def padded_2(block, sides, width):
    for axis, dim in sides:
        count = lax.axis_size(axis)
        forward = [(i, i + 1) for i in range(count - 1)]
        backward = [(target, source) for source, target in forward]
        low = lax.ppermute(
            lax.slice_in_dim(block, block.shape[dim] - width, None, axis=dim), axis, forward
        )
        high = lax.ppermute(lax.slice_in_dim(block, 0, width, axis=dim), axis, backward)
        block = jnp.concatenate([low, block, high], axis=dim)
    return block


def partner(block, axis, distance):
    count = lax.axis_size(axis)
    route = []
    for low in range(count):
        high = low | 1 << distance
        if high != low and high < count:
            route += [(low, high), (high, low)]
    return lax.ppermute(block, axis, route)


def shifted_diff(values, along_axis):
    padding = [(0, 0)] * values.ndim
    padding[along_axis] = (1, 1)
    padded = jnp.pad(values, padding)
    length_now = values.shape[along_axis]
    upper_part = lax.slice_in_dim(padded, 2, length_now + 2, 1, along_axis)
    lower_part = lax.slice_in_dim(padded, 0, length_now, 1, along_axis)
    return 0.5 * (upper_part - lower_part)


def layer_rgba(
    layer_below,
    center_layer,
    layer_above,
    light_dir,
    tf_center,
    tf_width,
    tf_height,
    tf_emission,
    depth_step,
):
    grad_z = 0.5 * (layer_above - layer_below)
    grad_y = shifted_diff(center_layer, 0)
    grad_x = shifted_diff(center_layer, 1)
    lighting = jnp.abs(
        grad_z[None] * light_dir[:, 0, None, None]
        + grad_y[None] * light_dir[:, 1, None, None]
        + grad_x[None] * light_dir[:, 2, None, None]
    )
    magnitude = jnp.sqrt(grad_x * grad_x + grad_y * grad_y + grad_z * grad_z + 1.0)
    shading = AMBIENT + DIFFUSE * lighting / magnitude[None]
    scaled = (center_layer[None, None] - tf_center[:, :, None, None]) / tf_width[:, :, None, None]
    bumps = jnp.exp(-scaled * scaled)
    density = jnp.sum(tf_height[:, :, None, None] * bumps, axis=1)
    weights = tf_height[:, :, None] * tf_emission
    tinted = jnp.einsum("vkc,vkhw->vchw", weights, bumps, precision=lax.Precision.HIGHEST)
    colour = depth_step * shading[:, None] * tinted
    opacity = 1.0 - jnp.exp(-depth_step * density)
    sample_rgba = jnp.concatenate([colour, opacity[:, None]], axis=1)
    return sample_rgba.reshape(sample_rgba.shape[0], 4, -1)


def over_ordered(lower_part, upper_part, flags):
    front_first = lower_part + (1.0 - lower_part[:, 3:4]) * upper_part
    back_first = upper_part + (1.0 - upper_part[:, 3:4]) * lower_part
    return jnp.where(flags, back_first, front_first)


def split_pair(values, along_axis):
    array_shape = values.shape
    new_shape = (
        array_shape[:along_axis] + (array_shape[along_axis] // 2, 2) + array_shape[along_axis + 1 :]
    )
    paired = values.reshape(new_shape)
    first_half = lax.index_in_dim(paired, 0, along_axis + 1, keepdims=False)
    second_half = lax.index_in_dim(paired, 1, along_axis + 1, keepdims=False)
    return (first_half, second_half)


def plain_body(volume, directions, light_dir, tf_center, tf_width, tf_height, tf_emission):
    depth_count = lax.axis_size("depth")
    wide_count = lax.axis_size("wide")
    slab_cells = volume.shape[0]
    depth_step = 1.0 / (slab_cells * depth_count * wide_count)
    view_count = light_dir.shape[0]
    pixel_count = volume.shape[1] * volume.shape[2]
    flags = jnp.repeat(directions == 1, volume.shape[2], axis=1)[:, None, :]
    padded = padded_2(volume, ((("depth", "wide"), 0),), 1)

    def advance(layer_index, composite):
        layers = lax.dynamic_slice_in_dim(padded, layer_index, 3, 0).astype(jnp.float32)
        sample_rgba = layer_rgba(
            layers[0],
            layers[1],
            layers[2],
            light_dir,
            tf_center,
            tf_width,
            tf_height,
            tf_emission,
            depth_step,
        )
        return over_ordered(composite, sample_rgba, flags)

    initial = jnp.zeros((view_count, 4, pixel_count), jnp.float32)
    slab_image = lax.fori_loop(0, slab_cells, advance, initial)
    block_pixels = pixel_count // (depth_count * wide_count)
    blocked = slab_image.reshape(view_count, 4, depth_count, wide_count, block_pixels)
    blocked_flags = flags.reshape(view_count, 1, depth_count, wide_count, block_pixels)
    wide_index = lax.axis_index("wide")
    depth_index = lax.axis_index("depth")
    merged = blocked
    merged_flags = blocked_flags
    for bit_number in range(wide_count.bit_length() - 1):
        own_bit = wide_index >> bit_number & 1
        first_half, second_half = split_pair(merged, 3)
        flag_first, flag_second = split_pair(merged_flags, 3)
        kept = jnp.where(own_bit == 0, first_half, second_half)
        outgoing = jnp.where(own_bit == 0, second_half, first_half)
        merged_flags = jnp.where(own_bit == 0, flag_first, flag_second)
        incoming = partner(outgoing, "wide", bit_number)
        merged = jnp.where(
            own_bit == 0,
            over_ordered(kept, incoming, merged_flags),
            over_ordered(incoming, kept, merged_flags),
        )
    range_image = jnp.squeeze(merged, 3)
    range_flags = jnp.squeeze(merged_flags, 3)
    merged = range_image
    merged_flags = range_flags
    for bit_number in range(depth_count.bit_length() - 1):
        own_bit = depth_index >> bit_number & 1
        first_half, second_half = split_pair(merged, 2)
        flag_first, flag_second = split_pair(merged_flags, 2)
        kept = jnp.where(own_bit == 0, first_half, second_half)
        outgoing = jnp.where(own_bit == 0, second_half, first_half)
        merged_flags = jnp.where(own_bit == 0, flag_first, flag_second)
        incoming = partner(outgoing, "depth", bit_number)
        merged = jnp.where(
            own_bit == 0,
            over_ordered(kept, incoming, merged_flags),
            over_ordered(incoming, kept, merged_flags),
        )
    final_block = jnp.squeeze(merged, 2)
    return final_block


MESH = pl.DeviceIdType.MESH
LOG2E = math.log2(math.e)
LANES = 256
ROWS = 16
LAG_CORE, LAG_Y, LAG_Z0, LAG_Z1, LAG_X = 2, 7, 12, 17, 21


def kernel(
    layer_total, chunks, groups,
    vol, dirs_in, light_in, center_in, width_in, height_in, tint_in,
    out,
    slabs, dirs, light, center, width, height, tint, in_sems,
    xf, halo, flagv, cst, obuf, cbuf, ysend, ybuf, zbuf, wbuf, xbuf, fin,
    halo_ss, halo_rs, send_sem, recv_sem, fin_ss, fin_rs,
):
    slab, rows, cols = vol.shape
    step = 1.0 / layer_total
    x = lax.axis_index("depth")
    w = lax.axis_index("wide")
    c = lax.rem(w, 2)
    y = lax.rem(lax.div(w, 2), 2)
    z0 = lax.rem(lax.div(w, 4), 2)
    z1 = lax.div(w, 8)
    me = x * 16 + w
    peers = (
        (x, w + 1 - 2 * c),
        (x, w + 2 - 4 * y),
        (x, w + 4 - 8 * z0),
        (x, w + 8 - 16 * z1),
        (1 - x, w),
    )
    core_peer, y_peer, z0_peer, z1_peer, x_peer = peers
    after = lax.rem(me + 1, 32)
    before = lax.rem(me + 31, 32)
    next_dev = (lax.div(after, 16), lax.rem(after, 16))
    prev_dev = (lax.div(before, 16), lax.rem(before, 16))
    has_prev = me > 0
    has_next = me < 31

    given = (
        (dirs_in, dirs), (light_in, light), (center_in, center), (width_in, width),
        (height_in, height), (tint_in, tint),
    )
    small = [pltpu.make_async_copy(a, b, in_sems.at[n]) for n, (a, b) in enumerate(given)]

    def slab_copy(z):
        return pltpu.make_async_copy(vol.at[z], slabs.at[z], in_sems.at[6 + z])

    barrier = pltpu.get_barrier_semaphore()
    for peer in peers + (next_dev, prev_dev):
        pl.semaphore_signal(barrier, inc=1, device_id=peer, device_id_type=MESH)
    for copy in small:
        copy.start()
    for z in range(slab):
        slab_copy(z).start()
    pl.semaphore_wait(barrier, 7)

    quarters = cols // LANES

    def up_copy(q):
        return pltpu.make_async_remote_copy(
            src_ref=vol.at[slab - 1, :, pl.ds(pl.multiple_of(q * LANES, LANES), LANES)],
            dst_ref=halo.at[0, q], send_sem=halo_ss.at[0, q], recv_sem=halo_rs.at[0, q],
            device_id=next_dev, device_id_type=MESH)

    def down_copy(q):
        return pltpu.make_async_remote_copy(
            src_ref=vol.at[0, :, pl.ds(pl.multiple_of(q * LANES, LANES), LANES)],
            dst_ref=halo.at[1, q], send_sem=halo_ss.at[1, q], recv_sem=halo_rs.at[1, q],
            device_id=prev_dev, device_id_type=MESH)

    for q in range(quarters):
        @pl.when(has_next)
        def _():
            up_copy(q).start()

        @pl.when(has_prev)
        def _():
            down_copy(q).start()

    for copy in small:
        copy.wait()
    for v in range(2):
        for k in range(4):
            full = lambda ref: jnp.full((8, 128), ref[v, k], jnp.float32)
            scale = math.sqrt(LOG2E) / full(width)
            cst[v * 15 + k] = scale
            cst[v * 15 + 4 + k] = scale * full(center)
            cst[v * 15 + 8 + k] = jnp.log(full(height) * (step * LOG2E)) * LOG2E
        for a in range(3):
            cst[v * 15 + 12 + a] = jnp.full((8, 128), DIFFUSE * light[v, a], jnp.float32)
    row_of = lax.broadcasted_iota(jnp.int32, (8, 128), 0)
    lane_of = lax.broadcasted_iota(jnp.int32, (8, 128), 1)

    def fill_flags(g, carry):
        for v in range(2):
            value = jnp.zeros((8, 128), jnp.float32)
            for i in range(8):
                value = jnp.where(row_of == i, dirs[v, g * 8 + i].astype(jnp.float32), value)
            flagv[v, g] = value
        return carry

    lax.fori_loop(0, rows // 8, fill_flags, 0)

    def pad(z, carry):
        slab_copy(z - 1).wait()
        xf[z, 0:8, :] = jnp.zeros((8, cols + 256), jnp.float32)
        xf[z, rows + 8:rows + 16, :] = jnp.zeros((8, cols + 256), jnp.float32)
        xf[z, 8:rows + 8, 0:128] = jnp.zeros((rows, 128), jnp.float32)
        xf[z, 8:rows + 8, cols + 128:cols + 256] = jnp.zeros((rows, 128), jnp.float32)

        def widen(b, inner):
            xf[z, pl.ds(pl.multiple_of(b * 16 + 8, 8), 16), 128:cols + 128] = slabs[
                z - 1, pl.ds(pl.multiple_of(b * 16, 16), 16), :
            ].astype(jnp.float32)
            return inner

        return lax.fori_loop(0, rows // 16, widen, carry)

    lax.fori_loop(1, slab + 1, pad, 0)

    def take_halo(side, place, present, copy, q):
        lanes = pl.ds(pl.multiple_of(q * LANES + 128, 128), LANES)

        @pl.when(present)
        def _():
            copy(q).wait_recv()
            xf[place, 8:rows + 8, lanes] = halo[side, q].astype(jnp.float32)

        @pl.when(jnp.logical_not(present))
        def _():
            xf[place, 8:rows + 8, lanes] = jnp.zeros((rows, LANES), jnp.float32)

    def place_of(k):
        return lax.rem(k, groups), lax.div(k, groups)

    def render(k):
        j, q = place_of(k)

        def tile(t, carry):
            h = lax.div(t, 2)
            p = lax.rem(t, 2)
            g = j * 2 + h
            r0 = pl.multiple_of(g * 8 + 8, 8)
            l0 = pl.multiple_of(q * LANES + p * 128 + 128, 128)
            here_rows, here_lanes = pl.ds(r0, 8), pl.ds(l0, 128)
            flags = [flagv[v, g] > 0.5 for v in range(2)]
            signs = [jnp.where(f, 1.0, -1.0) for f in flags]
            run = [jnp.zeros((8, 128), jnp.float32)] * 2
            sums = [[jnp.zeros((8, 128), jnp.float32)] * 4 for v in range(2)]
            for z in range(1, slab + 1):
                here = xf[z, here_rows, here_lanes]
                left = xf[z, here_rows, pl.ds(pl.multiple_of(l0 - 128, 128), 128)]
                right = xf[z, here_rows, pl.ds(pl.multiple_of(l0 + 128, 128), 128)]
                above = xf[z, pl.ds(pl.multiple_of(r0 - 8, 8), 8), here_lanes]
                below = xf[z, pl.ds(pl.multiple_of(r0 + 8, 8), 8), here_lanes]
                gz = xf[z + 1, here_rows, here_lanes] - xf[z - 1, here_rows, here_lanes]
                gx = pltpu.roll(jnp.where(lane_of == 0, right, here), 127, 1) - pltpu.roll(
                    jnp.where(lane_of == 127, left, here), 1, 1)
                gy = pltpu.roll(jnp.where(row_of == 0, below, here), 7, 0) - pltpu.roll(
                    jnp.where(row_of == 7, above, here), 1, 0)
                inverse = lax.rsqrt(gx * gx + gy * gy + (gz * gz + 4.0))
                for v in range(2):
                    dot = gz * cst[v * 15 + 12] + gy * cst[v * 15 + 13] + gx * cst[v * 15 + 14]
                    shade = jnp.abs(dot) * inverse + AMBIENT
                    bumps = []
                    for b in range(4):
                        u = here * cst[v * 15 + b] - cst[v * 15 + 4 + b]
                        bumps.append(jnp.exp2(cst[v * 15 + 8 + b] - u * u))
                    thick = (bumps[0] + bumps[1]) + (bumps[2] + bumps[3])
                    later = run[v] + signs[v] * thick
                    weight = jnp.exp2(jnp.where(flags[v], later, run[v])) * shade
                    run[v] = later
                    sums[v] = [s + weight * b for s, b in zip(sums[v], bumps)]
            lanes = pl.ds(pl.multiple_of(p * 128, 128), 128)
            for v in range(2):
                clear = jnp.exp2(-signs[v] * run[v])
                front = jnp.where(flags[v], clear, 1.0)
                scaled = [s * front for s in sums[v]]
                parts = []
                for ch in range(3):
                    total = scaled[0] * (tint[ch, v, 0] * (1.0 / LOG2E))
                    for b in range(1, 4):
                        total = total + scaled[b] * (tint[ch, v, b] * (1.0 / LOG2E))
                    parts.append(total)
                parts.append(clear)

                @pl.when(c == v)
                def _():
                    for ch in range(4):
                        cbuf[c, k, h, ch, :, lanes] = parts[ch]

                @pl.when(c != v)
                def _():
                    for ch in range(4):
                        obuf[k, h, ch, :, lanes] = parts[ch]
            return carry

        lax.fori_loop(0, 4, tile, 0)

    def merged(low, high, flag):
        lt, ut = low(3), high(3)
        p = jnp.where(flag, ut, 1.0)
        o = jnp.where(flag, 1.0, lt)
        return [p * low(ch) + o * high(ch) for ch in range(3)] + [lt * ut]

    def merge(low, high, flag_tile, store):
        for p in range(LANES // 128):
            s = slice(p * 128, p * 128 + 128)
            parts = merged(lambda ch: low[ch, :, s], lambda ch: high[ch, :, s], flag_tile > 0.5)
            for ch in range(4):
                store[ch, :, s] = parts[ch]

    def core_copy(k):
        return pltpu.make_async_remote_copy(
            src_ref=obuf.at[k], dst_ref=cbuf.at[c, k], send_sem=send_sem.at[0, k],
            recv_sem=recv_sem.at[0, k], device_id=core_peer, device_id_type=MESH)

    def y_copy(k):
        return pltpu.make_async_remote_copy(
            src_ref=ysend.at[k], dst_ref=ybuf.at[y, k], send_sem=send_sem.at[1, k],
            recv_sem=recv_sem.at[1, k], device_id=y_peer, device_id_type=MESH)

    def pass_on(buf, bit, stage, peer):
        return lambda k: pltpu.make_async_remote_copy(
            src_ref=buf.at[bit, k], dst_ref=buf.at[bit, k], send_sem=send_sem.at[stage, k],
            recv_sem=recv_sem.at[stage, k], device_id=peer, device_id_type=MESH)

    z0_copy = pass_on(zbuf, z0, 2, z0_peer)
    z1_copy = pass_on(wbuf, z1, 3, z1_peer)
    x_copy = pass_on(xbuf, x, 4, x_peer)

    def bits(k):
        j = lax.rem(k, groups)
        return lax.rem(j, 2), lax.rem(lax.div(j, 2), 2), lax.div(j, 4)

    def held(k):
        b0, b1, bx = bits(k)
        at0 = b0 == z0
        at1 = jnp.logical_and(at0, b1 == z1)
        return at0, at1, jnp.logical_and(at1, bx == x)

    def group_flag(k, half):
        return flagv[c, lax.rem(k, groups) * 2 + half]

    def inside(i, lag):
        return jnp.logical_and(i >= lag, i < chunks + lag)

    def advance(i, carry):
        @pl.when(jnp.logical_and(i < chunks, lax.rem(i, groups) == 0))
        def _():
            q = lax.div(i, groups)
            take_halo(0, 0, has_prev, up_copy, q)
            take_halo(1, slab + 1, has_next, down_copy, q)

        @pl.when(i < chunks)
        def _():
            render(i)
            core_copy(i).start()

        @pl.when(inside(i, LAG_CORE))
        def _():
            k = i - LAG_CORE
            core_copy(k).wait_recv()
            merge(cbuf.at[0, k, 1 - y], cbuf.at[1, k, 1 - y], group_flag(k, 1 - y), ysend.at[k])
            y_copy(k).start()
            merge(cbuf.at[0, k, y], cbuf.at[1, k, y], group_flag(k, y), ybuf.at[y, k])

        @pl.when(inside(i, LAG_Y))
        def _():
            k = i - LAG_Y
            y_copy(k).wait_recv()
            merge(ybuf.at[0, k], ybuf.at[1, k], group_flag(k, y), zbuf.at[z0, k])

            @pl.when(jnp.logical_not(held(k)[0]))
            def _():
                z0_copy(k).start()

        @pl.when(jnp.logical_and(inside(i, LAG_Z0), held(i + groups * 4 - LAG_Z0)[0]))
        def _():
            k = i - LAG_Z0
            z0_copy(k).wait_recv()
            merge(zbuf.at[0, k], zbuf.at[1, k], group_flag(k, y), wbuf.at[z1, k])

            @pl.when(jnp.logical_not(held(k)[1]))
            def _():
                z1_copy(k).start()

        @pl.when(jnp.logical_and(inside(i, LAG_Z1), held(i + groups * 4 - LAG_Z1)[1]))
        def _():
            k = i - LAG_Z1
            z1_copy(k).wait_recv()
            merge(wbuf.at[0, k], wbuf.at[1, k], group_flag(k, y), xbuf.at[x, k])

            @pl.when(jnp.logical_not(held(k)[2]))
            def _():
                x_copy(k).start()

        @pl.when(jnp.logical_and(inside(i, LAG_X), held(i + groups * 4 - LAG_X)[2]))
        def _():
            k = i - LAG_X
            x_copy(k).wait_recv()
            flag = group_flag(k, y) > 0.5
            for p in range(LANES // 128):
                s = slice(p * 128, p * 128 + 128)
                parts = merged(lambda ch: xbuf[0, k, ch, :, s], lambda ch: xbuf[1, k, ch, :, s], flag)
                parts[3] = 1.0 - parts[3]
                for r in range(8):
                    start = (r % 4) * cols + lax.div(k, groups) * LANES + p * 128
                    spot = pl.ds(pl.multiple_of(start, 128), 128)
                    for ch in range(4):
                        fin[r // 4, ch:ch + 1, spot] = parts[ch][r:r + 1, :]

        return carry

    lax.fori_loop(0, chunks + LAG_X, advance, 0)

    last = pltpu.make_async_remote_copy(
        src_ref=fin.at[1 - c], dst_ref=out.at[c], send_sem=fin_ss, recv_sem=fin_rs,
        device_id=core_peer, device_id_type=MESH)
    last.start()
    out[c] = fin[c]

    def settle(k, carry):
        core_copy(k).wait_send()
        y_copy(k).wait_send()
        at0, at1, at2 = held(k)

        @pl.when(jnp.logical_not(at0))
        def _():
            z0_copy(k).wait_send()

        @pl.when(jnp.logical_and(at0, jnp.logical_not(at1)))
        def _():
            z1_copy(k).wait_send()

        @pl.when(jnp.logical_and(at1, jnp.logical_not(at2)))
        def _():
            x_copy(k).wait_send()

        return carry

    lax.fori_loop(0, chunks, settle, 0)
    for q in range(quarters):
        @pl.when(has_next)
        def _():
            up_copy(q).wait_send()

        @pl.when(has_prev)
        def _():
            down_copy(q).wait_send()
    last.wait()


def fused_body(volume, directions, light_dir, tf_center, tf_width, tf_height, tf_emission):
    slab, rows, cols = volume.shape
    devices = lax.axis_size("depth") * lax.axis_size("wide")
    quarters = cols // LANES
    groups = rows // ROWS
    chunks = groups * quarters
    f32 = jnp.float32
    piece = (4, 8, LANES)
    vmem = pl.BlockSpec(memory_space=pltpu.VMEM)
    hbm = pl.BlockSpec(memory_space=pltpu.HBM)
    parameters = (
        directions, light_dir, tf_center, tf_width, tf_height, jnp.transpose(tf_emission, (2, 0, 1))
    )
    return pl.pallas_call(
        functools.partial(kernel, slab * devices, chunks, groups),
        out_shape=jax.ShapeDtypeStruct((2, 4, rows * cols // devices), f32),
        in_specs=[hbm] * 7,
        out_specs=vmem,
        scratch_shapes=[pltpu.VMEM(volume.shape, volume.dtype)]
        + [pltpu.SMEM(p.shape, p.dtype) for p in parameters]
        + [
            pltpu.SemaphoreType.DMA((6 + slab,)),
            pltpu.VMEM((slab + 2, rows + 16, cols + 256), f32),
            pltpu.VMEM((2, quarters, rows, LANES), volume.dtype),
            pltpu.VMEM((2, rows // 8, 8, 128), f32),
            pltpu.VMEM((30, 8, 128), f32),
            pltpu.VMEM((chunks, 2) + piece, f32),
            pltpu.VMEM((2, chunks, 2) + piece, f32),
            pltpu.VMEM((chunks,) + piece, f32),
            pltpu.VMEM((2, chunks) + piece, f32),
            pltpu.VMEM((2, chunks) + piece, f32),
            pltpu.VMEM((2, chunks) + piece, f32),
            pltpu.VMEM((2, chunks) + piece, f32),
            pltpu.VMEM((2, 4, rows * cols // devices), f32),
            pltpu.SemaphoreType.DMA((2, quarters)),
            pltpu.SemaphoreType.DMA((2, quarters)),
            pltpu.SemaphoreType.DMA((5, chunks)),
            pltpu.SemaphoreType.DMA((5, chunks)),
            pltpu.SemaphoreType.DMA,
            pltpu.SemaphoreType.DMA,
        ],
        compiler_params=pltpu.CompilerParams(
            collective_id=0, has_side_effects=True, vmem_limit_bytes=67043328
        ),
    )(volume, *parameters)


def body(volume, *parameters):
    slab, rows, cols = volume.shape
    fused = (
        lax.axis_size("depth") == 2
        and lax.axis_size("wide") == 16
        and rows == 128
        and cols % LANES == 0
    )
    return (fused_body if fused else plain_body)(volume, *parameters)


def solution(mesh):
    return jax.shard_map(
        body,
        mesh=mesh,
        in_specs=(P(("depth", "wide"), None, None), P(), P(), P(), P(), P(), P()),
        out_specs=P(None, None, ("depth", "wide")),
        check_vma=False,
    )
```
